256 devices in a mesh: site: 64 (over x, z, core), slab: 4 (over y).
Axes of the slice: x: 4, y: 4, z: 8, core: 2. Of those that a mesh axis runs over, the one named last changes fastest.
Arguments:
- jacobian: float32 [32768, 16384], P('site', 'slab'), may hold values from -3000 to 3000, as said below
- probe: float32 [16384, 256], P('slab'), may hold values from -0.046875 to 0.046875
Outputs:
- basis: float32 [32768, 256], P('site')
- projected: float32 [256, 16384], P('site', 'slab')
The draws below stay inside these ranges and needn't reach their ends.
Inputs may be any that keep to these rules, and one draw needn't show every extreme that they name: `jacobian`: finite real sensitivities.
All inputs are finite; a program needn't handle non-finite values.
Results may differ from the reference program's by a relative error of at most 0.00028.
Values sent between devices are 32-bit elements; how exact they have to be, the bound alone decides.
No kernel may reach another device: no remote copies, remote signals or barrier semaphores. Data moves between devices by JAX's collectives and lax.ppermute only.
A program may use at most 64 MiB of HBM per device.

```python
import jax
import jax.numpy as jnp
from jax import lax

CELLS = 16384
K = 256
ROWS = 32768


def draw_jacobian(key, part):
    key_z = jax.random.fold_in(key, 11)
    key_r = jax.random.fold_in(key, 12)
    key_c = jax.random.fold_in(key, 13)
    rows_pos = jnp.arange(ROWS, dtype=jnp.float32) / ROWS
    row_scale = 10.0 ** jax.random.uniform(key_r, (ROWS, 1), jnp.float32) * (3.0 ** rows_pos)[:, None]
    col_scale = 10.0 ** jax.random.uniform(key_c, (1, CELLS), jnp.float32)
    base = jnp.clip(jax.random.normal(key_z, (ROWS, CELLS), jnp.float32), -6.0, 6.0)
    return base * row_scale * col_scale


def steps_of(key, extent, pieces, least, largest):
    gain, own = 1.0, jax.random.fold_in(key, 6)
    for position, blocks in pieces:
        heights = jnp.exp(jax.random.uniform(jax.random.fold_in(own, position), (blocks,), jnp.float32, least / len(pieces), largest / len(pieces)))
        gain = gain * jnp.repeat(heights, extent[position] // blocks).reshape([-1 if axis == position else 1 for axis in range(len(extent))])
    return gain


def noise(rng, extent, width, most, shards=(), held_as=jnp.bfloat16):
    result = width * jax.random.normal(rng, extent, jnp.float32)
    if shards:
        result = result * steps_of(rng, extent, shards, -0.22, 0.18)
    return jnp.clip(result, -most, most).astype(held_as)


def setup_inputs(seed: int = 0) -> dict:
    splits = jax.random.split(jax.random.key(seed), 3)
    return {
        "jacobian": draw_jacobian(jax.random.fold_in(splits[2], 71), 0),
        "probe": noise(splits[1], (CELLS, K), CELLS ** -0.5, 0.046875, ((0, 4),), jnp.float32),
    }


def reference(jacobian, probe):
    sketch = jnp.dot(jacobian.astype(jnp.float32), probe.astype(jnp.float32), preferred_element_type=jnp.float32, precision=lax.Precision.HIGHEST)
    gram = jnp.dot(sketch.T.astype(jnp.float32), sketch.astype(jnp.float32), preferred_element_type=jnp.float32, precision=lax.Precision.HIGHEST)
    lower = jnp.linalg.cholesky(gram)
    ortho = jax.scipy.linalg.solve_triangular(lower, sketch.T, lower=True).T
    basis = jnp.sqrt(jnp.float32(ROWS)) * ortho
    projected = jnp.dot(ortho.T.astype(jnp.float32), jacobian.astype(jnp.float32), preferred_element_type=jnp.float32, precision=lax.Precision.HIGHEST)
    return (basis, projected)
```

```python
import functools

import jax
import jax.numpy as jnp
from jax import lax
from jax.experimental import pallas as pl
from jax.experimental.pallas import tpu as pltpu
from jax.sharding import Mesh
from jax.sharding import PartitionSpec as P

HIGH = lax.Precision.HIGH
HIGHEST = lax.Precision.HIGHEST
BLOCK = 128


def pairs(size, mask):
    return [(i, i ^ mask) for i in range(size)]


def swap(value, axis, mask):
    return lax.ppermute(value, axis, pairs(lax.axis_size(axis), mask))


def reciprocal(value):
    guess = pl.reciprocal(value, approx=True)
    guess = guess * (2.0 - value * guess)
    return guess * (2.0 - value * guess)


def eliminate(square):
    size = square.shape[0]
    wide = 2 * size
    count = size // 8
    same = lax.broadcasted_iota(jnp.int32, (size, size), 0) == lax.broadcasted_iota(jnp.int32, (size, size), 1)
    joined = jnp.concatenate([square, same.astype(jnp.float32)], axis=1)
    tiles = [joined[8 * i : 8 * i + 8] for i in range(count)]
    place = lax.broadcasted_iota(jnp.int32, (8, wide), 0)
    done = []
    for q in range(count):
        columns = [
            [jnp.broadcast_to(tiles[i][:, 8 * q + k : 8 * q + k + 1], (8, wide)) for i in range(q, count)]
            for k in range(8)
        ]
        pivots = None
        for k in range(8):
            pivot = jnp.broadcast_to(columns[k][0][k : k + 1], (8, wide))
            pivots = pivot if pivots is None else jnp.where(place >= k, pivot, pivots)
            inverse = reciprocal(pivot)
            factor = [c * inverse for c in columns[k]]
            factor[0] = jnp.where(place > k, factor[0], 0.0)
            for m in range(k + 1, 8):
                edge = jnp.broadcast_to(columns[m][0][k : k + 1], (8, wide))
                columns[m] = [c - f * edge for c, f in zip(columns[m], factor)]
            row = jnp.broadcast_to(tiles[q][k : k + 1], (8, wide))
            for i in range(q, count):
                tiles[i] = tiles[i] - factor[i - q] * row
        done.append(tiles[q] * lax.rsqrt(pivots))
    return jnp.concatenate([d[:, size:] for d in done], axis=0)


def factor_kernel(place_ref, *refs):
    parts, (whole_ref, split_ref, gram) = refs[:-3], refs[-3:]
    place = place_ref[0]
    rows, size = parts[0].shape
    for k, part in enumerate(parts):
        start = pl.multiple_of(jnp.bitwise_xor(place, k) * rows, rows)
        gram[pl.ds(start, rows), :] = part[...]
    blocks = size // BLOCK
    column = lax.broadcasted_iota(jnp.int32, (BLOCK, size), 1)
    row = lax.broadcasted_iota(jnp.int32, (BLOCK, size), 0)
    rest = [gram[BLOCK * i : BLOCK * (i + 1), :] for i in range(blocks)]
    for p in range(blocks):
        first = BLOCK * p
        inverse = eliminate(rest[p][:, first : first + BLOCK])
        inside = (column >= first) & (column < first + BLOCK)
        strip = jnp.where(inside, (column - first == row).astype(jnp.float32), rest[p])
        strip = jnp.dot(inverse, strip, precision=HIGHEST, preferred_element_type=jnp.float32)
        kept = jnp.where(column < first + BLOCK, strip, 0.0)
        whole_ref[first : first + BLOCK, :] = kept
        half = lax.broadcasted_iota(jnp.int32, (8, size), 0) < 4
        for t in range(BLOCK // 16):
            low, high = kept[16 * t : 16 * t + 8], kept[16 * t + 8 : 16 * t + 16]
            to = first // 2 + 8 * t
            split_ref[0, to : to + 8, :] = jnp.where(half, low, pltpu.roll(high, 4, 0))
            split_ref[1, to : to + 8, :] = jnp.where(half, pltpu.roll(low, 4, 0), high)
        if p + 1 < blocks:
            change = lax.dot_general(
                strip[:, first + BLOCK :],
                strip,
                (((0,), (0,)), ((), ())),
                precision=HIGHEST,
                preferred_element_type=jnp.float32,
            )
            for i in range(p + 1, blocks):
                at = BLOCK * (i - p - 1)
                rest[i] = jnp.where(inside, 0.0, rest[i]) - change[at : at + BLOCK]


def inverse_factor(parts, place):
    rows, size = parts[0].shape
    vmem = pl.BlockSpec(memory_space=pltpu.VMEM)
    return pl.pallas_call(
        factor_kernel,
        out_shape=(
            jax.ShapeDtypeStruct((size, size), jnp.float32),
            jax.ShapeDtypeStruct((2, size // 2, size), jnp.float32),
        ),
        in_specs=[pl.BlockSpec(memory_space=pltpu.SMEM)] + [vmem] * len(parts),
        out_specs=(vmem, vmem),
        scratch_shapes=[pltpu.VMEM((size, size), jnp.float32)],
        cost_estimate=pl.CostEstimate(flops=4 * size**3 * 50, bytes_accessed=12 * size * size, transcendentals=size),
        name="inverse_factor",
    )(place, *parts)


def group_sum(value, axis):
    one, two, three = (swap(value, axis, k) for k in (1, 2, 3))
    return (value + one) + (two + three)


def shards(jacobian, probe):
    width = probe.shape[1]
    columns = jacobian.shape[1]
    nx, nz, nc, ns = (lax.axis_size(a) for a in ("x", "z", "core", "slab"))
    total_rows = jacobian.shape[0] * nx * nz * nc
    slab, core = lax.axis_index("slab"), lax.axis_index("core")

    partial_value = jnp.dot(jacobian, probe, precision=HIGH, preferred_element_type=jnp.float32)
    middle = jacobian.shape[0] // 2
    top, bottom = partial_value[:middle], partial_value[middle:]
    top, bottom = top + swap(top, "slab", 1), bottom + swap(bottom, "slab", 3)
    top, bottom = top + swap(top, "slab", 3), bottom + swap(bottom, "slab", 1)
    sketch = jnp.concatenate([top, bottom], axis=0)

    gram = jnp.dot(sketch.T, sketch, precision=HIGHEST, preferred_element_type=jnp.float32)
    part = lax.dynamic_slice_in_dim(gram, slab * (width // ns), width // ns, 0)
    part = part + swap(part, "core", 1)
    part = group_sum(part, "x")
    part = group_sum(part, "z")
    part = part + swap(part, "z", 7)
    parts = [part] + [swap(part, "slab", k) for k in range(1, ns)]

    terms = jnp.dot(sketch.T, jacobian, precision=HIGH, preferred_element_type=jnp.float32)
    terms = terms.reshape(nc, width // nc, nx, nz, columns // (nx * nz)).transpose(0, 2, 3, 1, 4)
    mine = lax.dynamic_index_in_dim(terms, core, 0, keepdims=False)
    other = lax.dynamic_index_in_dim(terms, 1 - core, 0, keepdims=False)
    mine = mine + swap(other, "core", 1)
    mine = lax.all_to_all(mine, "x", 0, 0).sum(0)
    mine = lax.all_to_all(mine, "z", 0, 0).sum(0)
    across = swap(mine, "core", 1)
    terms = jnp.where(core == 0, jnp.stack([mine, across]), jnp.stack([across, mine])).reshape(width, -1)

    whole, split = inverse_factor(parts, slab.reshape(1))
    basis = jnp.sqrt(jnp.float32(total_rows)) * lax.dot_general(
        sketch, whole, (((1,), (1,)), ((), ())), precision=HIGHEST, preferred_element_type=jnp.float32
    )
    rows = lax.dynamic_index_in_dim(split, core, 0, keepdims=False)
    owned = jnp.dot(rows, terms, precision=HIGHEST, preferred_element_type=jnp.float32)
    owned = owned.reshape(nx * nz, width // (nx * nz * nc), -1)
    owned = lax.all_to_all(owned, ("x", "z"), 0, 0)
    return basis, owned.transpose(1, 0, 2).reshape(owned.shape[1], columns)


def solution(mesh):
    grid = Mesh(mesh.devices.reshape(4, 8, 2, 4), ("x", "z", "core", "slab"))
    site = ("x", "z", "core")
    return jax.shard_map(
        shards,
        mesh=grid,
        in_specs=(P(site, "slab"), P("slab", None)),
        out_specs=(P(site, None), P(site, "slab")),
        check_vma=False,
    )
```

```python
import jax
import jax.numpy as jnp
from jax import lax
from jax.experimental import pallas as pl
from jax.experimental.pallas import tpu as pltpu
from jax.sharding import Mesh
from jax.sharding import PartitionSpec as P

HIGH = lax.Precision.HIGH
HIGHEST = lax.Precision.HIGHEST
BLOCK = 128


def pairs(size, mask):
    return [(i, i ^ mask) for i in range(size)]


def swap(value, axis, mask):
    return lax.ppermute(value, axis, pairs(lax.axis_size(axis), mask))


def reciprocal(value):
    guess = pl.reciprocal(value, approx=True)
    guess = guess * (2.0 - value * guess)
    return guess * (2.0 - value * guess)


def eliminate(square):
    size = square.shape[0]
    wide = 2 * size
    count = size // 8
    same = lax.broadcasted_iota(jnp.int32, (size, size), 0) == lax.broadcasted_iota(jnp.int32, (size, size), 1)
    joined = jnp.concatenate([square, same.astype(jnp.float32)], axis=1)
    tiles = [joined[8 * i : 8 * i + 8] for i in range(count)]
    place = lax.broadcasted_iota(jnp.int32, (8, wide), 0)
    done = []
    for q in range(count):
        columns = [
            [jnp.broadcast_to(tiles[i][:, 8 * q + k : 8 * q + k + 1], (8, wide)) for i in range(q, count)]
            for k in range(8)
        ]
        pivots = None
        for k in range(8):
            pivot = jnp.broadcast_to(columns[k][0][k : k + 1], (8, wide))
            pivots = pivot if pivots is None else jnp.where(place >= k, pivot, pivots)
            inverse = reciprocal(pivot)
            factor = [c * inverse for c in columns[k]]
            factor[0] = jnp.where(place > k, factor[0], 0.0)
            for m in range(k + 1, 8):
                edge = jnp.broadcast_to(columns[m][0][k : k + 1], (8, wide))
                columns[m] = [c - f * edge for c, f in zip(columns[m], factor)]
            row = jnp.broadcast_to(tiles[q][k : k + 1], (8, wide))
            for i in range(q, count):
                tiles[i] = tiles[i] - factor[i - q] * row
        done.append(tiles[q] * lax.rsqrt(pivots))
    return jnp.concatenate([d[:, size:] for d in done], axis=0)


def factor_kernel(place_ref, *refs):
    parts, (whole_ref, split_ref, gram) = refs[:-3], refs[-3:]
    place = place_ref[0]
    rows, size = parts[0].shape
    for k, part in enumerate(parts):
        start = pl.multiple_of(jnp.bitwise_xor(place, k) * rows, rows)
        gram[pl.ds(start, rows), :] = part[...]
    blocks = size // BLOCK
    column = lax.broadcasted_iota(jnp.int32, (BLOCK, size), 1)
    row = lax.broadcasted_iota(jnp.int32, (BLOCK, size), 0)
    rest = [gram[BLOCK * i : BLOCK * (i + 1), :] for i in range(blocks)]
    for p in range(blocks):
        first = BLOCK * p
        inverse = eliminate(rest[p][:, first : first + BLOCK])
        inside = (column >= first) & (column < first + BLOCK)
        strip = jnp.where(inside, (column - first == row).astype(jnp.float32), rest[p])
        strip = jnp.dot(inverse, strip, precision=HIGHEST, preferred_element_type=jnp.float32)
        kept = jnp.where(column < first + BLOCK, strip, 0.0)
        whole_ref[first : first + BLOCK, :] = kept
        half = lax.broadcasted_iota(jnp.int32, (8, size), 0) < 4
        for t in range(BLOCK // 16):
            low, high = kept[16 * t : 16 * t + 8], kept[16 * t + 8 : 16 * t + 16]
            to = first // 2 + 8 * t
            split_ref[0, to : to + 8, :] = jnp.where(half, low, pltpu.roll(high, 4, 0))
            split_ref[1, to : to + 8, :] = jnp.where(half, pltpu.roll(low, 4, 0), high)
        if p + 1 < blocks:
            change = lax.dot_general(
                strip[:, first + BLOCK :],
                strip,
                (((0,), (0,)), ((), ())),
                precision=HIGHEST,
                preferred_element_type=jnp.float32,
            )
            for i in range(p + 1, blocks):
                at = BLOCK * (i - p - 1)
                rest[i] = jnp.where(inside, 0.0, rest[i]) - change[at : at + BLOCK]


def inverse_factor(parts, place):
    _, size = parts[0].shape
    vmem = pl.BlockSpec(memory_space=pltpu.VMEM)
    return pl.pallas_call(
        factor_kernel,
        out_shape=(
            jax.ShapeDtypeStruct((size, size), jnp.float32),
            jax.ShapeDtypeStruct((2, size // 2, size), jnp.float32),
        ),
        in_specs=[pl.BlockSpec(memory_space=pltpu.SMEM)] + [vmem] * len(parts),
        out_specs=(vmem, vmem),
        scratch_shapes=[pltpu.VMEM((size, size), jnp.float32)],
        cost_estimate=pl.CostEstimate(flops=4 * size**3 * 50, bytes_accessed=12 * size * size, transcendentals=size),
        compiler_params=pltpu.CompilerParams(vmem_limit_bytes=12 << 20),
        name="inverse_factor",
    )(place, *parts)


def group_sum(value, axis):
    one, three, two = (swap(value, axis, k) for k in (1, 3, 2))
    return (value + one) + (two + three)


def compute(jacobian, probe):
    width = probe.shape[1]
    columns = jacobian.shape[1]
    nx, nz, nc, ns = (lax.axis_size(a) for a in ("x", "z", "core", "slab"))
    total_rows = jacobian.shape[0] * nx * nz * nc
    slab, core = lax.axis_index("slab"), lax.axis_index("core")

    middle = jacobian.shape[0] // 2
    partial_value = jnp.dot(jacobian, probe, precision=HIGH, preferred_element_type=jnp.float32)
    top, bottom = partial_value[:middle], partial_value[middle:]
    top = top + swap(top, "slab", 1)
    bottom = bottom + swap(bottom, "slab", 3)
    top = top + swap(top, "slab", 3)
    bottom = bottom + swap(bottom, "slab", 1)
    sketch = jnp.concatenate([top, bottom], axis=0)

    gram = jnp.dot(sketch.T, sketch, precision=HIGHEST, preferred_element_type=jnp.float32)
    part = lax.dynamic_slice_in_dim(gram, slab * (width // ns), width // ns, 0)
    part = part + swap(part, "core", 1)
    part = group_sum(part, "x")
    part = group_sum(part, "z")
    part = part + swap(part, "z", 7)
    parts = [part] + [swap(part, "slab", k) for k in range(1, ns)]

    terms = jnp.dot(sketch.T, jacobian, precision=HIGH, preferred_element_type=jnp.float32)
    terms = terms.reshape(nc, width // nc, nx, nz, columns // (nx * nz)).transpose(0, 2, 3, 1, 4)
    mine = lax.dynamic_index_in_dim(terms, core, 0, keepdims=False)
    other = lax.dynamic_index_in_dim(terms, 1 - core, 0, keepdims=False)
    mine = mine + swap(other, "core", 1)
    mine = lax.all_to_all(mine, "x", 0, 0).sum(0)
    mine = lax.all_to_all(mine, "z", 0, 0).sum(0)
    across = swap(mine, "core", 1)
    terms = jnp.where(core == 0, jnp.stack([mine, across]), jnp.stack([across, mine])).reshape(width, -1)

    whole, split = inverse_factor(parts, slab.reshape(1))
    basis = jnp.sqrt(jnp.float32(total_rows)) * lax.dot_general(
        sketch, whole, (((1,), (1,)), ((), ())), precision=HIGHEST, preferred_element_type=jnp.float32
    )
    rows = lax.dynamic_index_in_dim(split, core, 0, keepdims=False)
    owned = jnp.dot(rows, terms, precision=HIGHEST, preferred_element_type=jnp.float32)
    owned = owned.reshape(nx * nz, width // (nx * nz * nc), -1)
    owned = lax.all_to_all(owned, ("x", "z"), 0, 0)
    return basis, owned.transpose(1, 0, 2).reshape(owned.shape[1], columns)


def solution(mesh):
    grid = Mesh(mesh.devices.reshape(4, 8, 2, 4), ("x", "z", "core", "slab"))
    site = ("x", "z", "core")
    return jax.shard_map(
        compute,
        mesh=grid,
        in_specs=(P(site, "slab"), P("slab", None)),
        out_specs=(P(site, None), P(site, "slab")),
        check_vma=False,
    )
```

```python
import functools

import jax
import jax.numpy as jnp
from jax import lax
from jax.experimental import pallas as pl
from jax.experimental.pallas import tpu as pltpu
from jax.sharding import Mesh
from jax.sharding import PartitionSpec as P

HIGH = lax.Precision.HIGH
HIGHEST = lax.Precision.HIGHEST
BLOCK = 128


def pairs(size, mask):
    return [(i, i ^ mask) for i in range(size)]


def swap(value, axis, mask):
    return lax.ppermute(value, axis, pairs(lax.axis_size(axis), mask))


def reciprocal(value):
    guess = pl.reciprocal(value, approx=True)
    guess = guess * (2.0 - value * guess)
    return guess * (2.0 - value * guess)


def eliminate(square):
    size = square.shape[0]
    wide = 2 * size
    count = size // 8
    same = lax.broadcasted_iota(jnp.int32, (size, size), 0) == lax.broadcasted_iota(jnp.int32, (size, size), 1)
    joined = jnp.concatenate([square, same.astype(jnp.float32)], axis=1)
    tiles = [joined[8 * i : 8 * i + 8] for i in range(count)]
    place = lax.broadcasted_iota(jnp.int32, (8, wide), 0)
    done = []
    for q in range(count):
        columns = [
            [jnp.broadcast_to(tiles[i][:, 8 * q + k : 8 * q + k + 1], (8, wide)) for i in range(q, count)]
            for k in range(8)
        ]
        pivots = None
        for k in range(8):
            pivot = jnp.broadcast_to(columns[k][0][k : k + 1], (8, wide))
            pivots = pivot if pivots is None else jnp.where(place >= k, pivot, pivots)
            inverse = reciprocal(pivot)
            factor = [c * inverse for c in columns[k]]
            factor[0] = jnp.where(place > k, factor[0], 0.0)
            for m in range(k + 1, 8):
                edge = jnp.broadcast_to(columns[m][0][k : k + 1], (8, wide))
                columns[m] = [c - f * edge for c, f in zip(columns[m], factor)]
            row = jnp.broadcast_to(tiles[q][k : k + 1], (8, wide))
            for i in range(q, count):
                tiles[i] = tiles[i] - factor[i - q] * row
        done.append(tiles[q] * lax.rsqrt(pivots))
    return jnp.concatenate([d[:, size:] for d in done], axis=0)


def factor_kernel(place_ref, *refs):
    parts, (whole_ref, split_ref, gram) = refs[:-3], refs[-3:]
    place = place_ref[0]
    rows, size = parts[0].shape
    for k, part in enumerate(parts):
        start = pl.multiple_of(jnp.bitwise_xor(place, k) * rows, rows)
        gram[pl.ds(start, rows), :] = part[...]
    blocks = size // BLOCK
    column = lax.broadcasted_iota(jnp.int32, (BLOCK, size), 1)
    row = lax.broadcasted_iota(jnp.int32, (BLOCK, size), 0)
    rest = [gram[BLOCK * i : BLOCK * (i + 1), :] for i in range(blocks)]
    for p in range(blocks):
        first = BLOCK * p
        inverse = eliminate(rest[p][:, first : first + BLOCK])
        inside = (column >= first) & (column < first + BLOCK)
        strip = jnp.where(inside, (column - first == row).astype(jnp.float32), rest[p])
        strip = jnp.dot(inverse, strip, precision=HIGHEST, preferred_element_type=jnp.float32)
        kept = jnp.where(column < first + BLOCK, strip, 0.0)
        whole_ref[first : first + BLOCK, :] = kept
        half = lax.broadcasted_iota(jnp.int32, (8, size), 0) < 4
        for t in range(BLOCK // 16):
            low, high = kept[16 * t : 16 * t + 8], kept[16 * t + 8 : 16 * t + 16]
            to = first // 2 + 8 * t
            split_ref[0, to : to + 8, :] = jnp.where(half, low, pltpu.roll(high, 4, 0))
            split_ref[1, to : to + 8, :] = jnp.where(half, pltpu.roll(low, 4, 0), high)
        if p + 1 < blocks:
            change = lax.dot_general(
                strip[:, first + BLOCK :],
                strip,
                (((0,), (0,)), ((), ())),
                precision=HIGHEST,
                preferred_element_type=jnp.float32,
            )
            for i in range(p + 1, blocks):
                at = BLOCK * (i - p - 1)
                rest[i] = jnp.where(inside, 0.0, rest[i]) - change[at : at + BLOCK]


def inverse_factor(parts, place):
    _, size = parts[0].shape
    vmem = pl.BlockSpec(memory_space=pltpu.VMEM)
    return pl.pallas_call(
        factor_kernel,
        out_shape=(
            jax.ShapeDtypeStruct((size, size), jnp.float32),
            jax.ShapeDtypeStruct((2, size // 2, size), jnp.float32),
        ),
        in_specs=[pl.BlockSpec(memory_space=pltpu.SMEM)] + [vmem] * len(parts),
        out_specs=(vmem, vmem),
        scratch_shapes=[pltpu.VMEM((size, size), jnp.float32)],
        cost_estimate=pl.CostEstimate(flops=4 * size**3 * 50, bytes_accessed=12 * size * size, transcendentals=size),
        compiler_params=pltpu.CompilerParams(vmem_limit_bytes=12 << 20),
        name="inverse_factor",
    )(place, *parts)


def owned_kernel(core_ref, split_ref, mine_ref, across_ref, out_ref):
    core = core_ref[0]
    rows = split_ref[core]
    half = mine_ref.shape[0]
    mine, across = mine_ref[...], across_ref[...]
    dot = functools.partial(jnp.dot, precision=HIGHEST, preferred_element_type=jnp.float32)
    upper, lower = jnp.where(core == 0, mine, across), jnp.where(core == 0, across, mine)
    value = dot(rows[:, :half], upper) + dot(rows[:, half:], lower)
    step = out_ref.shape[1]
    for t in range(out_ref.shape[0]):
        out_ref[t] = value[step * t : step * t + step]


def owned_of(split, mine, across, core, sites):
    vmem = pl.BlockSpec(memory_space=pltpu.VMEM)
    rows = split.shape[1]
    return pl.pallas_call(
        owned_kernel,
        out_shape=jax.ShapeDtypeStruct((sites, rows // sites, mine.shape[1]), jnp.float32),
        in_specs=[pl.BlockSpec(memory_space=pltpu.SMEM), vmem, vmem, vmem],
        out_specs=vmem,
        compiler_params=pltpu.CompilerParams(vmem_limit_bytes=12 << 20),
        cost_estimate=pl.CostEstimate(flops=12 * rows * rows * 256, bytes_accessed=1 << 19, transcendentals=0),
        name="owned_rows",
    )(core.reshape(1), split, mine, across)


def group_sum(value, axis):
    one, three, two = (swap(value, axis, k) for k in (1, 3, 2))
    return (value + one) + (two + three)


def compute(jacobian, probe):
    width = probe.shape[1]
    columns = jacobian.shape[1]
    nx, nz, nc, ns = (lax.axis_size(a) for a in ("x", "z", "core", "slab"))
    total_rows = jacobian.shape[0] * nx * nz * nc
    slab, core = lax.axis_index("slab"), lax.axis_index("core")

    middle = jacobian.shape[0] // 2
    partial_value = jnp.dot(jacobian, probe, precision=HIGH, preferred_element_type=jnp.float32)
    top, bottom = partial_value[:middle], partial_value[middle:]
    top = top + swap(top, "slab", 1)
    bottom = bottom + swap(bottom, "slab", 3)
    top = top + swap(top, "slab", 3)
    bottom = bottom + swap(bottom, "slab", 1)
    sketch = jnp.concatenate([top, bottom], axis=0)

    gram = jnp.dot(sketch.T, sketch, precision=HIGHEST, preferred_element_type=jnp.float32)
    part = lax.dynamic_slice_in_dim(gram, slab * (width // ns), width // ns, 0)
    part = part + swap(part, "core", 1)
    part = group_sum(part, "x")
    part = group_sum(part, "z")
    part = part + swap(part, "z", 7)
    parts = [part] + [swap(part, "slab", k) for k in range(1, ns)]

    terms = jnp.dot(sketch.T, jacobian, precision=HIGH, preferred_element_type=jnp.float32)
    terms = terms.reshape(nc, width // nc, nx, nz, columns // (nx * nz)).transpose(0, 2, 3, 1, 4)
    mine = lax.dynamic_index_in_dim(terms, core, 0, keepdims=False)
    other = lax.dynamic_index_in_dim(terms, 1 - core, 0, keepdims=False)
    mine = mine + swap(other, "core", 1)
    mine = lax.all_to_all(mine, "x", 0, 0).sum(0)
    mine = lax.all_to_all(mine, "z", 0, 0).sum(0)
    across = swap(mine, "core", 1)
    whole, split = inverse_factor(parts, slab.reshape(1))
    basis = jnp.sqrt(jnp.float32(total_rows)) * lax.dot_general(
        sketch, whole, (((1,), (1,)), ((), ())), precision=HIGHEST, preferred_element_type=jnp.float32
    )
    owned = owned_of(split, mine, across, core, nx * nz)
    owned = lax.all_to_all(owned, ("x", "z"), 0, 0)
    return basis, owned.transpose(1, 0, 2).reshape(owned.shape[1], columns)


def solution(mesh):
    grid = Mesh(mesh.devices.reshape(4, 8, 2, 4), ("x", "z", "core", "slab"))
    site = ("x", "z", "core")
    return jax.shard_map(
        compute,
        mesh=grid,
        in_specs=(P(site, "slab"), P("slab", None)),
        out_specs=(P(site, None), P(site, "slab")),
        check_vma=False,
    )
```
